256 devices in a mesh: fit: 8 (over z_hi, x), pair: 16 (over y, z_lo), blk: 2 (over core).
Axes of the slice: x: 4, y: 4, z: 8 (z_hi: 2, z_lo: 4; z = z_hi * 4 + z_lo), core: 2. Of those that a mesh axis runs over, the one named last changes fastest.
Arguments:
- left_factor: float32 [128, 512, 2048], P('pair', 'blk', 'fit'), may hold values from -2 to 2
- right_factor: float32 [128, 512, 2048], P('pair', None, 'fit'), may hold values from -2 to 2
- amplitudes: float32 [128, 512, 512], P(('pair', 'fit'), 'blk'), may hold values from -6 to 6
- domain_trans: float32 [128, 512, 512], P(('pair', 'fit')), may hold values from -0.25 to 0.25
- vir_energy: float32 [128, 512], P(('pair', 'fit')), may hold values from 0.5 to 3
- occ_energy: float32 [128], P(('pair', 'fit')), may hold values from 0.2 to 1
- coupling: float32 [128, 4], P(('pair', 'fit')), may hold values from -4 to 4
- neighbours: int32 [128, 4], P(('pair', 'fit')), may hold values from 0 to 127, as said below
- dom_blocks: int32 [128], P(('pair', 'fit')), may hold values from 1 to 4
Outputs:
- new_amplitudes: float32 [128, 512, 512], P(('pair', 'fit'), 'blk')
- density_fit: float32 [128, 2048], P('pair', 'fit')
The draws below stay inside these ranges and needn't reach their ends.
Inputs may be any that keep to these rules, and one draw needn't show every extreme that they name: `neighbours`: with s(p) = p // 8, each entry names a pair p' with (p') % 8 equal to that of the listing pair p, and s(p') equal to s(p), s(p) + 1, s(p) - 1 or s(p) + 8, modulo 16; entries may repeat.
All inputs are finite; a program needn't handle non-finite values.
Results may differ from the reference program's by a relative error of at most 0.000068.
Values sent between devices are 32-bit elements; how exact they have to be, the bound alone decides.
No kernel may reach another device: no remote copies, remote signals or barrier semaphores. Data moves between devices by JAX's collectives and lax.ppermute only.
A program may use at most 64 MiB of HBM per device.

```python
import math
import jax
import jax.numpy as jnp
from jax import lax

V = 512
NAUX = 2048
NB = 4
PAIR_DEV = 1
PAIRS = 128
N_FIT = 8
N_PAIR = 16


def draw_neighbours(key, part):
    total = PAIR_DEV * N_FIT * N_PAIR
    pair_ids = jnp.arange(total, dtype=jnp.int32)
    own_shard = pair_ids // (N_FIT * PAIR_DEV)
    offsets = jnp.array([0, 1, N_PAIR - 1, N_PAIR // 2], dtype=jnp.int32)
    choose = jax.random.randint(jax.random.fold_in(key, 1), (total, NB), 0, 4, dtype=jnp.int32)
    choose = choose.at[0, 0].set(0).at[total - 1, 0].set(0)
    shard = (own_shard[:, None] + offsets[choose]) % N_PAIR
    local = jax.random.randint(jax.random.fold_in(key, 3), (total, NB), 0, PAIR_DEV, dtype=jnp.int32)
    local = local.at[0, 0].set(0).at[total - 1, 0].set(PAIR_DEV - 1)
    fit_slot = pair_ids // PAIR_DEV % N_FIT
    return (shard * N_FIT + fit_slot[:, None]) * PAIR_DEV + local


def touch_ends(result, rng, low, largest):
    longest = result.shape.index(max(result.shape))
    spots = []
    for shift in (0, 1):
        where = [jax.random.randint(jax.random.fold_in(rng, axis), (), 0, length) for axis, length in enumerate(result.shape)]
        where[longest] = (where[longest] + shift) % result.shape[longest]
        spots.append(tuple(where))
    return result.at[spots[0]].set(low).at[spots[1]].set(largest)


def shard_levels(stream_key, extent, split, smallest, largest):
    gain, own = 1.0, jax.random.fold_in(stream_key, 6)
    for dim, shards_of in split:
        heights = jnp.exp(jax.random.uniform(jax.random.fold_in(own, dim), (shards_of,), jnp.float32, smallest / len(split), largest / len(split)))
        gain = gain * jnp.repeat(heights, extent[dim] // shards_of).reshape([-1 if axis == dim else 1 for axis in range(len(extent))])
    return gain


def scatter_about(stream_key, dims, scale, bound, cuts=(), kind=jnp.bfloat16):
    values = scale * jax.random.normal(stream_key, dims, jnp.float32)
    if cuts:
        values = values * shard_levels(stream_key, dims, cuts, -0.22, 0.18)
    return jnp.clip(values, -bound, bound).astype(kind)


def setup_inputs(seed: int = 0) -> dict:
    arg_keys = jax.random.split(jax.random.key(seed), 10)
    return {
        "left_factor": scatter_about(arg_keys[0], (PAIRS, V, NAUX), (NAUX ** -0.25), 2.0, ((0, 16), (1, 2), (2, 8)), jnp.float32),
        "right_factor": scatter_about(arg_keys[1], (PAIRS, V, NAUX), (NAUX ** -0.25), 2.0, ((0, 16), (2, 8)), jnp.float32),
        "amplitudes": scatter_about(arg_keys[2], (PAIRS, V, V), 0.5, 6.0, ((0, 128), (1, 2)), jnp.float32),
        "domain_trans": scatter_about(arg_keys[3], (PAIRS, V, V), V ** -0.5, 0.25, ((0, 128),), jnp.float32),
        "vir_energy": jnp.clip(jnp.exp(math.log(3.0) - 1.7917595 * jax.random.uniform(arg_keys[4], (PAIRS, V), jnp.float32) ** shard_levels(arg_keys[4], (PAIRS, V), ((0, 128),), -0.2, 0.2)), 0.5, 3.0),
        "occ_energy": jnp.clip(0.2 + 0.8 * jax.random.uniform(arg_keys[5], (PAIRS,), jnp.float32) ** shard_levels(arg_keys[5], (PAIRS,), ((0, 128),), -0.2, 0.2), 0.2, 1.0),
        "coupling": scatter_about(arg_keys[6], (PAIRS, NB), 1.0, 4.0, ((0, 128),), jnp.float32),
        "neighbours": draw_neighbours(jax.random.fold_in(arg_keys[9], 71), 0),
        "dom_blocks": touch_ends(jax.random.randint(arg_keys[8], (PAIRS,), 1, 5), jax.random.fold_in(arg_keys[8], 1), 1, 4).astype(jnp.int32),
    }


def reference(left_factor, right_factor, amplitudes, domain_trans, vir_energy, occ_energy, coupling, neighbours, dom_blocks):
    precise = lax.Precision.HIGHEST
    integrals = jnp.einsum("pad,pbd->pab", left_factor, right_factor, precision=precise)
    mixed = jnp.einsum("pab,pcb->pac", amplitudes, domain_trans, precision=precise)
    summed = jnp.zeros(amplitudes.shape, jnp.float32)
    for column in range(NB):
        summed = summed + coupling[:, column, None, None] * mixed[neighbours[:, column]]
    correction = jnp.einsum("pac,pcb->pab", summed, domain_trans, precision=precise)
    denominator = vir_energy[:, :, None] + vir_energy[:, None, :] + occ_energy[:, None, None]
    residual = integrals + denominator * amplitudes - correction
    limit = dom_blocks * (V // 4)
    position = jnp.arange(V, dtype=jnp.int32)
    inside = (position[None, :, None] < limit[:, None, None]) & (position[None, None, :] < limit[:, None, None])
    updated = amplitudes - 0.7 * residual / denominator
    new_amplitudes = jnp.where(inside, updated, jnp.zeros_like(updated))
    product = jnp.einsum("pab,pbq->paq", new_amplitudes, right_factor, precision=precise)
    density_fit = jnp.sum(left_factor * product, axis=1)
    return new_amplitudes, density_fit
```

```python
import functools

import jax
import jax.numpy as jnp
from jax import lax
from jax.experimental import pallas as pl
from jax.experimental.pallas import tpu as pltpu
from jax.sharding import PartitionSpec as P


F32 = jnp.float32
NT = (((1,), (1,)), ((), ()))
NN = (((1,), (0,)), ((), ()))


def halves(v):
    top = v.astype(jnp.bfloat16)
    return top, (v - top.astype(F32)).astype(jnp.bfloat16)


def dot3(a, b, dims):
    a_top, a_low = a
    b_top, b_low = b
    dot = functools.partial(lax.dot_general, dimension_numbers=dims, preferred_element_type=F32)
    return (dot(a_low, b_top) + dot(a_top, b_low)) + dot(a_top, b_top)


def matmul_kernel(a_ref, b_ref, out_ref, *, dims):
    out_ref[...] = dot3(halves(a_ref[...]), halves(b_ref[...]), dims)


def matmul(a, b, dims, shape):
    flops = 6 * a.shape[0] * a.shape[1] * shape[1]
    return pl.pallas_call(
        functools.partial(matmul_kernel, dims=dims),
        out_shape=jax.ShapeDtypeStruct(shape, F32),
        cost_estimate=pl.CostEstimate(flops=flops, bytes_accessed=4 * (a.size + b.size + shape[0] * shape[1]), transcendentals=0),
    )(a, b)


def correction_kernel(weights, m0, m1, m2, m3, d_ref, out_ref):
    total = weights[0] * m0[...] + weights[1] * m1[...]
    total += weights[2] * m2[...] + weights[3] * m3[...]
    out_ref[...] = dot3(halves(total), halves(d_ref[...]), NN)


def partial_integral(core, left, right, packs, others, out_ref):
    out_ref[...] = dot3(halves(left), halves(right), NT)
    half = right.shape[0] // 2
    mine = pl.ds(pl.multiple_of(core * half, half), half)
    yours = pl.ds(pl.multiple_of((1 - core) * half, half), half)
    for pack, other in zip(packs, others):
        rows = pack.shape[0] - half
        piece = halves(pack[0:rows, :])
        out_ref[:, mine] += dot3(piece, halves(pack[rows:, :]), NT)
        out_ref[:, yours] += dot3(piece, halves(other[...]), NT)


def integral_kernel(where, left, right, k1, k2, k3, o1, o2, o3, out_ref):
    partial_integral(where[0], left[0], right[0], (k1, k2, k3), (o1, o2, o3), out_ref)


def denominators(rows_ref, columns_ref, occ):
    return rows_ref[...] + columns_ref[...] + occ


def residual_kernel(where, occ, left, right, k1, k2, k3, o1, o2, o3, amp, corr, rows, columns, out_ref):
    partial_integral(where[0], left[0], right[0], (k1, k2, k3), (o1, o2, o3), out_ref)
    below = denominators(rows, columns, occ[0])
    residual = out_ref[...] + below * amp[...] - corr[...]
    out_ref[...] = amp[...] - 0.7 * residual / below


def density_kernel(where, occ, left, right, k1, k2, k3, o1, o2, o3, early, late, rows, columns, new_ref, sums_ref):
    core, limit = where[0], where[2]
    below = denominators(rows, columns, occ[0])
    shape = early.shape
    row = core * shape[0] + lax.broadcasted_iota(jnp.int32, shape, 0)
    column = lax.broadcasted_iota(jnp.int32, shape, 1)
    updated = early[...] - 0.7 * late[...] / below
    new = jnp.where((row < limit) & (column < limit), updated, 0.0)
    new_ref[...] = new
    half = right.shape[1] // 2
    product = dot3(halves(new), halves(right[0]), NN)
    sums_ref[0:1, :] = jnp.sum(left[0] * product, axis=0, keepdims=True)
    mine = halves(new_ref[:, pl.ds(pl.multiple_of(core * half, half), half)])
    yours = halves(new_ref[:, pl.ds(pl.multiple_of((1 - core) * half, half), half)])
    for step, (pack, other) in enumerate(((k1, o1), (k2, o2), (k3, o3)), 1):
        depth = shape[0]
        product = dot3(mine, halves(pack[depth:, :]), NN) + dot3(yours, halves(other[...]), NN)
        sums_ref[step : step + 1, :] = jnp.sum(pack[0:depth, :] * product, axis=0, keepdims=True)


def call(kernel, scalars, left, right, packs, others, extras, outs, flops):
    def whole(a):
        return pl.BlockSpec(a.shape, lambda i, *s: (0,) * len(a.shape))

    arrays = (*packs, *others, *extras)
    return pl.pallas_call(
        kernel,
        grid_spec=pltpu.PrefetchScalarGridSpec(
            num_scalar_prefetch=len(scalars),
            grid=(1,),
            in_specs=[
                pl.BlockSpec((1, *left.shape[1:]), lambda i, where, *s: (where[1], 0, 0)),
                pl.BlockSpec((1, *right.shape[1:]), lambda i, where, *s: (where[1], 0, 0)),
                *[whole(a) for a in arrays],
            ],
            out_specs=[whole(o) for o in outs],
        ),
        out_shape=outs,
        cost_estimate=pl.CostEstimate(flops=flops, bytes_accessed=4 * sum(a.size for a in arrays), transcendentals=0),
    )(*scalars, left, right, *arrays)


def body(left, right, amplitudes, domain_trans, vir_energy, occ_energy, coupling, neighbours, dom_blocks):
    fit_count, pair_count = lax.axis_size("fit"), lax.axis_size("pair")
    ring = fit_count // 2
    rows, width, depth = left.shape[1], right.shape[1], left.shape[2]
    core, fit, shard = (lax.axis_index(name) for name in ("blk", "fit", "pair"))
    side, place = fit // ring, fit % ring
    amp, trans = amplitudes[0], domain_trans[0]
    swap = [(0, 1), (1, 0)]
    across = [(f, (f + ring) % fit_count) for f in range(fit_count)]

    def shifted(by):
        return [(s * ring + i, s * ring + (i + by) % ring) for s in range(2) for i in range(ring)]

    def from_shard(value, by):
        return lax.ppermute(value, "pair", [((s + by) % pair_count, s) for s in range(pair_count)])

    mixed = matmul(amp, trans, NT, (rows, width))
    offsets = (0, 1, pair_count - 1, pair_count // 2)
    blocks = [mixed] + [from_shard(mixed, by) for by in offsets[1:]]
    relative = (neighbours[0] // fit_count - shard + pair_count) % pair_count
    weights = jnp.stack([jnp.sum(jnp.where(relative == by, coupling[0], 0.0)) for by in offsets])
    facts = jnp.concatenate([vir_energy[0], occ_energy, dom_blocks.astype(F32), jnp.zeros((126,), F32)])
    facts = jnp.stack([facts, lax.ppermute(facts, "fit", across)])

    def pair_facts(which):
        vir = facts[which, :width]
        row_energy = lax.dynamic_slice_in_dim(vir, core * rows, rows, 0)
        limit = (facts[which, width + 1].astype(jnp.int32)) * (width // 4)
        return row_energy[:, None], vir[None, :], facts[which, width : width + 1], limit

    def exchange(group):
        packs, others = [], []
        for by in range(1, ring):
            slot = group * ring + (place + by) % ring
            pack = jnp.concatenate([
                lax.dynamic_slice(left, (slot, 0, 0), (1, rows, depth))[0],
                lax.dynamic_slice(right, (slot, core * (width // 2), 0), (1, width // 2, depth))[0],
            ])
            packs.append(lax.ppermute(pack, "fit", shifted(by)))
        for pack in packs:
            others.append(lax.ppermute(pack[rows:], "blk", swap))
        return packs, others

    theirs = exchange(1 - side)
    mine = exchange(side)
    my_slot, their_slot = fit, (1 - side) * ring + place
    block = jax.ShapeDtypeStruct((rows, width), F32)
    sums = jax.ShapeDtypeStruct((ring, depth), F32)
    flops = 6 * rows * width * depth * ring

    def where(slot, limit):
        return jnp.stack([core, slot, limit]).astype(jnp.int32)

    my_rows, my_columns, my_occ, my_limit = pair_facts(0)
    their_rows, their_columns, their_occ, their_limit = pair_facts(1)
    (their_part,) = call(integral_kernel, (where(their_slot, their_limit),), left, right, *theirs, (), [block], flops)
    my_late = lax.ppermute(their_part, "fit", across)
    (corr,) = pl.pallas_call(
        correction_kernel,
        in_specs=[pl.BlockSpec(memory_space=pltpu.SMEM)] + [pl.BlockSpec(memory_space=pltpu.VMEM)] * 5,
        out_shape=[block],
        cost_estimate=pl.CostEstimate(flops=6 * rows * width * width, bytes_accessed=24 * rows * width, transcendentals=0),
    )(weights, *blocks, trans)
    (my_early,) = call(residual_kernel, (where(my_slot, my_limit), my_occ), left, right, *mine, (amp, corr, my_rows, my_columns), [block], flops)
    their_early = lax.ppermute(my_early, "fit", across)
    new, my_sums = call(density_kernel, (where(my_slot, my_limit), my_occ), left, right, *mine, (my_early, my_late, my_rows, my_columns), [block, sums], flops)
    _, their_sums = call(density_kernel, (where(their_slot, their_limit), their_occ), left, right, *theirs, (their_early, their_part, their_rows, their_columns), [block, sums], flops)
    both = jnp.stack([my_sums, their_sums], axis=1)
    both = both + lax.ppermute(both, "blk", swap)
    parts = [both[0]] + [lax.ppermute(both[by], "fit", shifted(-by)) for by in range(1, ring)]
    density = jnp.zeros((2, ring, depth), F32)
    for by, part in enumerate(parts):
        at = (place + by) % ring
        density = jnp.where((jnp.arange(ring) == at)[None, :, None], part[:, None, :], density)
    density = jnp.where(side == 0, density, density[::-1])
    return new[None], density.reshape(fit_count, depth)


def solution(mesh):
    placed = (
        P("pair", "blk", "fit"),
        P("pair", None, "fit"),
        P(("pair", "fit"), "blk", None),
        P(("pair", "fit"), None, None),
        P(("pair", "fit"), None),
        P(("pair", "fit")),
        P(("pair", "fit"), None),
        P(("pair", "fit"), None),
        P(("pair", "fit")),
    )
    return jax.shard_map(
        body,
        mesh=mesh,
        in_specs=placed,
        out_specs=(P(("pair", "fit"), "blk", None), P("pair", "fit")),
        check_vma=False,
    )
```

```python
import functools

import jax
import jax.numpy as jnp
from jax import lax
from jax.experimental import pallas as pl
from jax.experimental.pallas import tpu as pltpu
from jax.sharding import PartitionSpec as P


F32 = jnp.float32
NT = (((1,), (1,)), ((), ()))
NN = (((1,), (0,)), ((), ()))
ANY = pl.BlockSpec(memory_space=pltpu.HBM)
SCALARS = pl.BlockSpec(memory_space=pltpu.SMEM)
WHOLE = pl.BlockSpec(memory_space=pltpu.VMEM)
LIMIT = pltpu.CompilerParams(vmem_limit_bytes=16 << 20)
SEGMENT = 4
EXTRA = 8


def halves(v):
    top = v.astype(jnp.bfloat16)
    return top, (v - top.astype(F32)).astype(jnp.bfloat16)


def dot3(a, b, dims):
    a_top, a_low = a
    b_top, b_low = b
    dot = functools.partial(lax.dot_general, dimension_numbers=dims, preferred_element_type=F32)
    return (dot(a_low, b_top) + dot(a_top, b_low)) + dot(a_top, b_top)


def seat(ring, own):
    fit = lax.axis_index("fit")
    side = fit // ring
    return fit % ring, (side if own else 1 - side) * ring


def fill_packs(ring, own, left, right, outs, sems):
    place, first = seat(ring, own)
    rows = left.shape[1]
    half = right.shape[1] // 2
    part = half // 2
    start = lax.axis_index("blk") * half
    copies = []
    for by in range(1, ring):
        slot = first + (place + by) % ring
        long, short = outs[by - 1], outs[ring - 2 + by]
        for i, (source, to) in enumerate((
            (left.at[slot], long.at[0:rows]),
            (right.at[slot, pl.ds(pl.multiple_of(start, part), part)], long.at[rows : rows + part]),
            (right.at[slot, pl.ds(pl.multiple_of(start + part, part), part)], short),
        )):
            copies.append(pltpu.make_async_copy(source, to, sems.at[by - 1, i]))
    for copy in copies:
        copy.start()
    return copies


def pack_kernel(ring, own, left, right, _, *refs):
    for copy in fill_packs(ring, own, left, right, refs[:-1], refs[-1]):
        copy.wait()


def head_kernel(ring, left, right, amp, trans, *refs):
    *packs, mixed, amp_here, trans_here, sems, own_sems = refs
    reads = [
        pltpu.make_async_copy(amp, amp_here, own_sems.at[0]),
        pltpu.make_async_copy(trans, trans_here, own_sems.at[1]),
    ]
    for read in reads:
        read.start()
    copies = fill_packs(ring, False, left, right, packs, sems)
    for read in reads:
        read.wait()
    mixed[...] = dot3(halves(amp_here[...]), halves(trans_here[...]), NT)
    for copy in copies:
        copy.wait()


def gather_kernel(*refs):
    *sources, out_ref = refs
    part = out_ref.shape[1]
    for i, source in enumerate(sources):
        out_ref[i] = source[source.shape[0] - part :, :]


def fetch(ring, own, left, right, left_here, right_here, sems):
    place, first = seat(ring, own)
    copies = [
        pltpu.make_async_copy(left.at[first + place], left_here, sems.at[0]),
        pltpu.make_async_copy(right.at[first + place], right_here, sems.at[1]),
    ]
    for copy in copies:
        copy.start()
    return copies


def columns(part, which):
    core = lax.axis_index("blk")
    return [pl.ds(pl.multiple_of((2 * c + which) * part, part), part) for c in (core, 1 - core)]


def integral_kernel(ring, own, which, left, right, *refs):
    (*packs, rights, out_ref, left_here, right_here, sems) = refs
    copies = fetch(ring, own, left, right, left_here, right_here, sems)
    rows = left_here.shape[0]
    part = rights.shape[1]
    total = None
    for i, pack in enumerate(packs):
        term = dot3(halves(pack[0:rows, :]), halves(rights[i]), NT)
        total = term if total is None else total + term
    for copy in copies:
        copy.wait()
    own_left = halves(left_here[...])
    mine, yours = columns(part, which)
    out_ref[:, 0:part] = total + dot3(own_left, halves(right_here[mine, :]), NT)
    out_ref[:, part:] = dot3(own_left, halves(right_here[yours, :]), NT)


def finished(part_ref, packs, others):
    rows, part = part_ref.shape[0], others.shape[1]
    total = part_ref[:, part:]
    for i, pack in enumerate(packs):
        total += dot3(halves(pack[0:rows, :]), halves(others[i]), NT)
    return jnp.concatenate([part_ref[:, 0:part], total], axis=1)


def finish_kernel(part_ref, *refs):
    *packs, others, out_ref = refs
    out_ref[...] = finished(part_ref, packs, others)


def denominators(facts, rows):
    width = facts.shape[1]
    column = jnp.broadcast_to(facts[1:2, 0:rows], (128, rows)).T
    return jnp.concatenate([column] * (width // 128), axis=1) + facts[0:1, :] + facts[2:3, 0:1]


def residual_kernel(which, occ, dom, part_ref, *refs):
    *packs, others, amp, corr, vir, out_ref = refs
    rows, width = amp.shape
    part = others.shape[1]
    spots = columns(part, which)
    core = lax.axis_index("blk")
    out_ref[rows:, :] = jnp.concatenate([
        jnp.concatenate([vir[:, spot] for spot in spots], axis=1),
        vir[:, pl.ds(pl.multiple_of(core * rows, rows), rows)],
        jnp.full((1, 2 * part), occ[0], F32),
        jnp.full((1, 2 * part), (dom[0] * (width // 4)).astype(F32), F32),
        jnp.zeros((EXTRA - 4, 2 * part), F32),
    ])
    below = denominators(out_ref.at[rows : rows + EXTRA], rows)
    old = jnp.concatenate([amp[:, spot] for spot in spots], axis=1)
    fixed = below * old - jnp.concatenate([corr[:, spot] for spot in spots], axis=1)
    residual = finished(part_ref, packs, others) + fixed
    out_ref[0:rows, :] = old - 0.7 * residual / below


def density_kernel(ring, own, which, left, right, *refs):
    refs = list(refs)
    take = lambda n: [refs.pop(0) for _ in range(n)]
    longs = take(ring - 1)
    shorts = take(ring - 1) if 1 in which else []
    others = dict(zip(which, take(len(which))))
    early, late = take(len(which)), take(len(which))
    before = None if 0 in which else take(1)[0]
    new_ref = take(1)[0] if own else None
    sums_ref, left_here, right_here, sems = refs
    copies = fetch(ring, own, left, right, left_here, right_here, sems)
    rows, part = late[0].shape[0], late[0].shape[1] // 2
    core = lax.axis_index("blk")
    row = (core * rows + lax.broadcasted_iota(jnp.int32, (rows, 2 * part), 0)).astype(F32)
    lane = lax.broadcasted_iota(jnp.int32, (rows, 2 * part), 1)
    new = {}
    for w, block, term in zip(which, early, late):
        facts = block.at[rows : rows + EXTRA]
        below = denominators(facts, rows)
        offset = jnp.where(lane < part, 2 * core * part, (1 - 2 * core) * part) + w * part
        column = (lane + offset).astype(F32)
        limit = facts[3:4, 0:1]
        updated = block[0:rows, :] - 0.7 * term[...] / below
        value = jnp.where((row < limit) & (column < limit), updated, 0.0)
        if own:
            mine, yours = columns(part, w)
            new_ref[:, mine] = value[:, 0:part]
            new_ref[:, yours] = value[:, part:]
        new[w] = halves(value)

    def add_up(spot, lefts, rights):
        product = None
        for w, value in new.items():
            term = dot3(value, halves(rights(w)), NN)
            product = term if product is None else product + term
        sums_ref[spot : spot + 1, :] = jnp.sum(lefts * product, axis=0, keepdims=True)

    for i, long in enumerate(longs):
        add_up(
            i + 1,
            long[0:rows, :],
            lambda w: jnp.concatenate([long[rows:, :] if w == 0 else shorts[i][...], others[w][i]], axis=0),
        )
    for copy in copies:
        copy.wait()
    add_up(0, left_here[...], lambda w: jnp.concatenate([right_here[spot, :] for spot in columns(part, w)], axis=0))
    if before is not None:
        sums_ref[...] += before[...]


def correction_kernel(pairs_per_shard, shards, neighbours, coupling, mixed, up, down, wrap, far, d_ref, out_ref):
    shard = lax.axis_index("pair")

    def weight(by):
        total = jnp.float32(0)
        for k in range(neighbours.shape[0]):
            apart = (neighbours[k] // pairs_per_shard - shard + shards) % shards
            total += jnp.where(apart == by, coupling[k], 0.0)
        return total

    above, below = weight(1), weight(shards - 1)
    spot = shard % SEGMENT
    ends = jnp.where(spot == SEGMENT - 1, above, jnp.where(spot == 0, below, 0.0))
    total = weight(0) * mixed[...] + above * up[...] + below * down[...]
    total += ends * wrap[...] + weight(shards // 2) * far[...]
    out_ref[...] = dot3(halves(total), halves(d_ref[...]), NN)


def vmem(*arrays):
    return [pltpu.with_memory_space_constraint(a, pltpu.VMEM) for a in arrays]


def hbm(*arrays):
    return [pltpu.with_memory_space_constraint(a, pltpu.HBM) for a in arrays]


def cost(flops, moved):
    return pl.CostEstimate(flops=flops, bytes_accessed=moved, transcendentals=0)


def body(left, right, amplitudes, domain_trans, vir_energy, occ_energy, coupling, neighbours, dom_blocks):
    fit_count, pair_count = lax.axis_size("fit"), lax.axis_size("pair")
    ring = fit_count // 2
    rows, width, depth = left.shape[1], right.shape[1], left.shape[2]
    fit = lax.axis_index("fit")
    side, place = fit // ring, fit % ring
    amp, trans = amplitudes[0], domain_trans[0]
    swap = [(0, 1), (1, 0)]
    across = [(f, (f + ring) % fit_count) for f in range(fit_count)]
    block = jax.ShapeDtypeStruct((rows, width), F32)
    sums = jax.ShapeDtypeStruct((ring, depth), F32)

    def shifted(by):
        return [(s * ring + i, s * ring + (i + by) % ring) for s in range(2) for i in range(ring)]

    def send(value, axis, pairs):
        return lax.ppermute(value, axis, pairs)

    def from_shards(value, sources):
        return send(value, "pair", [(source % pair_count, to) for to, source in sources])

    part = width // 4
    packs = [jax.ShapeDtypeStruct((rows + part, depth), F32)] * (ring - 1) + [jax.ShapeDtypeStruct((part, depth), F32)] * (ring - 1)
    pack_sems = pltpu.SemaphoreType.DMA((ring - 1, 3))
    some = jax.ShapeDtypeStruct((rows, 2 * part), F32)
    some_long = jax.ShapeDtypeStruct((rows + EXTRA, 2 * part), F32)
    edge = jax.ShapeDtypeStruct((ring - 1, part, depth), F32)

    def spread(values):
        return [send(value, "fit", shifted(by)) for by, value in enumerate(values, 1)]

    def swapped(values):
        gathered = pl.pallas_call(
            gather_kernel,
            in_specs=[WHOLE] * len(values),
            out_specs=WHOLE,
            out_shape=edge,
            compiler_params=LIMIT,
            cost_estimate=cost(0, 8 * edge.size),
        )(*vmem(*values))
        return gathered, send(gathered, "blk", swap)

    def work(kernel, own, which, factors, extras, outs):
        return pl.pallas_call(
            functools.partial(kernel, ring, own, which),
            in_specs=[ANY] * 2 + [WHOLE] * (len(factors) + len(extras)),
            out_specs=[WHOLE] * len(outs),
            out_shape=outs,
            scratch_shapes=[
                pltpu.VMEM((rows, depth), F32),
                pltpu.VMEM((width, depth), F32),
                pltpu.SemaphoreType.DMA((2,)),
            ],
            compiler_params=LIMIT,
            cost_estimate=cost(3 * rows * width * depth * ring, 2 * ring * depth * (rows + width)),
        )(*hbm(left, right), *vmem(*factors, *extras))

    *sent, mixed = pl.pallas_call(
        functools.partial(head_kernel, ring),
        in_specs=[ANY] * 4,
        out_specs=[WHOLE] * (2 * ring - 1),
        out_shape=packs + [block],
        scratch_shapes=[pltpu.VMEM(amp.shape, F32), pltpu.VMEM(trans.shape, F32), pack_sems, pltpu.SemaphoreType.DMA((2,))],
        compiler_params=LIMIT,
        cost_estimate=cost(6 * rows * width * width, 32 * rows * width),
    )(*hbm(left, right, amp, trans))
    their_longs, their_shorts = spread(sent[: ring - 1]), spread(sent[ring - 1 :])
    shards = range(pair_count)
    near = [
        from_shards(mixed, [(s, s + 1) for s in shards if s % SEGMENT < SEGMENT - 1]),
        from_shards(mixed, [(s, s - 1) for s in shards if s % SEGMENT > 0]),
        from_shards(mixed, [(s, s + 1) for s in shards if s % SEGMENT == SEGMENT - 1] + [(s, s - 1) for s in shards if s % SEGMENT == 0]),
        from_shards(mixed, [(s, s + pair_count // 2) for s in shards]),
    ]
    sent = pl.pallas_call(
        functools.partial(pack_kernel, ring, True),
        in_specs=[ANY] * 3,
        out_specs=[WHOLE] * len(packs),
        out_shape=packs,
        scratch_shapes=[pack_sems],
        compiler_params=LIMIT,
        cost_estimate=cost(0, 24 * rows * width),
    )(*hbm(left, right), mixed)
    my_longs, my_shorts = spread(sent[: ring - 1]), spread(sent[ring - 1 :])
    (corr,) = pl.pallas_call(
        functools.partial(correction_kernel, fit_count, pair_count),
        in_specs=[SCALARS] * 2 + [WHOLE] * 6,
        out_specs=[WHOLE],
        out_shape=[block],
        compiler_params=LIMIT,
        cost_estimate=cost(6 * rows * width * width, 28 * rows * width),
    )(neighbours[0], coupling[0], mixed, *near, trans)

    their_others, their_parts, my_late = [], [], []
    for which, source in enumerate((their_longs, their_shorts)):
        gathered, other = swapped(source)
        (started,) = work(integral_kernel, False, which, (*their_longs, gathered), (), [some])
        done = pl.pallas_call(
            finish_kernel,
            in_specs=[WHOLE] * (2 + len(their_longs)),
            out_specs=WHOLE,
            out_shape=some,
            compiler_params=LIMIT,
            cost_estimate=cost(2 * rows * width * depth, 16 * rows * width),
        )(started, *vmem(*their_longs, other))
        their_others.append(other)
        their_parts.append(done)
        my_late.append(send(done, "fit", across))
    my_others, my_early, their_early = [], [], []
    for which, source in enumerate((my_longs, my_shorts)):
        gathered, other = swapped(source)
        (started,) = work(integral_kernel, True, which, (*my_longs, gathered), (), [some])
        done = pl.pallas_call(
            functools.partial(residual_kernel, which),
            in_specs=[SCALARS] * 2 + [WHOLE] * (5 + len(my_longs)),
            out_specs=WHOLE,
            out_shape=some_long,
            compiler_params=LIMIT,
            cost_estimate=cost(2 * rows * width * depth, 24 * rows * width),
        )(occ_energy, dom_blocks, started, *vmem(*my_longs, other), amp, corr, vir_energy)
        my_others.append(other)
        my_early.append(done)
        their_early.append(send(done, "fit", across))
    new, my_sums = work(
        density_kernel, True, (0, 1), (*my_longs, *my_shorts, *my_others), (*my_early, *my_late), [block, sums]
    )
    (their_sums,) = work(
        density_kernel, False, (0,), (*their_longs, their_others[0]), (their_early[0], their_parts[0]), [sums]
    )
    (their_sums,) = work(
        density_kernel, False, (1,), (*their_longs, *their_shorts, their_others[1]),
        (their_early[1], their_parts[1], their_sums), [sums],
    )
    both = jnp.stack([my_sums, their_sums], axis=1)
    both = both + lax.ppermute(both, "blk", swap)
    parts = [both[0]] + [lax.ppermute(both[by], "fit", shifted(-by)) for by in range(1, ring)]
    density = jnp.zeros((2, ring, depth), F32)
    for by, part in enumerate(parts):
        at = (place + by) % ring
        density = jnp.where((jnp.arange(ring) == at)[None, :, None], part[:, None, :], density)
    density = jnp.where(side == 0, density, density[::-1])
    return new[None], density.reshape(fit_count, depth)


def solution(mesh):
    placed = (
        P("pair", "blk", "fit"),
        P("pair", None, "fit"),
        P(("pair", "fit"), "blk", None),
        P(("pair", "fit"), None, None),
        P(("pair", "fit"), None),
        P(("pair", "fit")),
        P(("pair", "fit"), None),
        P(("pair", "fit"), None),
        P(("pair", "fit")),
    )
    return jax.shard_map(
        lambda *args: body(*args),
        mesh=mesh,
        in_specs=placed,
        out_specs=(P(("pair", "fit"), "blk", None), P("pair", "fit")),
        check_vma=False,
    )
```

```python
import functools

import jax
import jax.numpy as jnp
from jax import lax
from jax.experimental import pallas as pl
from jax.experimental.pallas import tpu as pltpu
from jax.sharding import PartitionSpec as P


F32 = jnp.float32
NT = (((1,), (1,)), ((), ()))
NN = (((1,), (0,)), ((), ()))
ANY = pl.BlockSpec(memory_space=pltpu.HBM)
SCALARS = pl.BlockSpec(memory_space=pltpu.SMEM)
WHOLE = pl.BlockSpec(memory_space=pltpu.VMEM)
LIMIT = pltpu.CompilerParams(vmem_limit_bytes=16 << 20)
SEGMENT = 4
EXTRA = 8


def halves(v):
    top = v.astype(jnp.bfloat16)
    return top, (v - top.astype(F32)).astype(jnp.bfloat16)


def dot3(a, b, dims):
    a_top, a_low = a
    b_top, b_low = b
    dot = functools.partial(lax.dot_general, dimension_numbers=dims, preferred_element_type=F32)
    return (dot(a_low, b_top) + dot(a_top, b_low)) + dot(a_top, b_top)


def seat(ring, own):
    fit = lax.axis_index("fit")
    side = fit // ring
    return fit % ring, (side if own else 1 - side) * ring


def fill_packs(ring, own, left, right, outs, sems):
    place, first = seat(ring, own)
    rows = left.shape[1]
    half = right.shape[1] // 2
    part = half // 2
    start = lax.axis_index("blk") * half
    copies = []
    for by in range(1, ring):
        slot = first + (place + by) % ring
        long, short = outs[by - 1], outs[ring - 2 + by]
        for i, (source, to) in enumerate((
            (left.at[slot], long.at[0:rows]),
            (right.at[slot, pl.ds(pl.multiple_of(start, part), part)], long.at[rows : rows + part]),
            (right.at[slot, pl.ds(pl.multiple_of(start + part, part), part)], short),
        )):
            copies.append(pltpu.make_async_copy(source, to, sems.at[by - 1, i]))
    for copy in copies:
        copy.start()
    return copies


def pack_kernel(ring, own, occ, dom, left, right, vir, _, *refs):
    *packs, facts, sems = refs
    copies = fill_packs(ring, own, left, right, packs, sems)
    rows, width = left.shape[1], vir.shape[1]
    part = width // 4
    core = lax.axis_index("blk")
    for which in range(facts.shape[0]):
        facts[which] = jnp.concatenate([
            jnp.concatenate([vir[:, spot] for spot in columns(part, which)], axis=1),
            vir[:, pl.ds(pl.multiple_of(core * rows, rows), rows)],
            jnp.full((1, 2 * part), occ[0], F32),
            jnp.full((1, 2 * part), (dom[0] * part).astype(F32), F32),
            jnp.concatenate([vir[:, spot] for spot in columns(part, 1)], axis=1),
            jnp.zeros((EXTRA - 5, 2 * part), F32),
        ])
    for copy in copies:
        copy.wait()


def head_kernel(ring, left, right, amp, trans, *refs):
    *packs, mixed, amp_here, trans_here, sems, own_sems = refs
    reads = [
        pltpu.make_async_copy(amp, amp_here, own_sems.at[0]),
        pltpu.make_async_copy(trans, trans_here, own_sems.at[1]),
    ]
    for read in reads:
        read.start()
    copies = fill_packs(ring, False, left, right, packs, sems)
    for read in reads:
        read.wait()
    mixed[...] = dot3(halves(amp_here[...]), halves(trans_here[...]), NT)
    for copy in copies:
        copy.wait()


def gather_kernel(*refs):
    *sources, out_ref = refs
    part = out_ref.shape[1]
    for i, source in enumerate(sources):
        out_ref[i] = source[source.shape[0] - part :, :]


def fetch(ring, own, left, right, left_here, right_here, sems):
    place, first = seat(ring, own)
    copies = [
        pltpu.make_async_copy(left.at[first + place], left_here, sems.at[0]),
        pltpu.make_async_copy(right.at[first + place], right_here, sems.at[1]),
    ]
    for copy in copies:
        copy.start()
    return copies


def columns(part, which):
    core = lax.axis_index("blk")
    return [pl.ds(pl.multiple_of((2 * c + which) * part, part), part) for c in (core, 1 - core)]


def integral_kernel(ring, own, which, left, right, *refs):
    (*packs, rights, out_ref, left_here, right_here, sems) = refs
    copies = fetch(ring, own, left, right, left_here, right_here, sems)
    rows = left_here.shape[0]
    part = rights.shape[1]
    total = None
    for i, pack in enumerate(packs):
        term = dot3(halves(pack[0:rows, :]), halves(rights[i]), NT)
        total = term if total is None else total + term
    for copy in copies:
        copy.wait()
    own_left = halves(left_here[...])
    mine, yours = columns(part, which)
    out_ref[:, 0:part] = total + dot3(own_left, halves(right_here[mine, :]), NT)
    out_ref[:, part:] = dot3(own_left, halves(right_here[yours, :]), NT)


def finished(part_ref, packs, others):
    rows, part = part_ref.shape[0], others.shape[1]
    total = part_ref[:, part:]
    for i, pack in enumerate(packs):
        total += dot3(halves(pack[0:rows, :]), halves(others[i]), NT)
    return jnp.concatenate([part_ref[:, 0:part], total], axis=1)


def finish_kernel(part_ref, *refs):
    *packs, others, out_ref = refs
    out_ref[...] = finished(part_ref, packs, others)


def denominators(facts, rows, at=0):
    width = facts.shape[1]
    column = jnp.broadcast_to(facts[1:2, 0:rows], (128, rows)).T
    return jnp.concatenate([column] * (width // 128), axis=1) + facts[at : at + 1, :] + facts[2:3, 0:1]


def inside(facts, rows, part, which):
    core = lax.axis_index("blk")
    row = (core * rows + lax.broadcasted_iota(jnp.int32, (rows, 2 * part), 0)).astype(F32)
    lane = lax.broadcasted_iota(jnp.int32, (rows, 2 * part), 1)
    offset = jnp.where(lane < part, 2 * core * part, (1 - 2 * core) * part) + which * part
    limit = facts[3:4, 0:1]
    return (row < limit) & ((lane + offset).astype(F32) < limit)


def residual_kernel(which, part_ref, *refs):
    *packs, others, amp, corr, facts, out_ref = refs
    rows = amp.shape[0]
    spots = columns(others.shape[1], which)
    out_ref[rows:, :] = facts[which]
    below = denominators(facts.at[which], rows)
    old = jnp.concatenate([amp[:, spot] for spot in spots], axis=1)
    fixed = below * old - jnp.concatenate([corr[:, spot] for spot in spots], axis=1)
    residual = finished(part_ref, packs, others) + fixed
    out_ref[0:rows, :] = old - 0.7 * residual / below


def density_kernel(ring, own, which, left, right, *refs):
    refs = list(refs)
    take = lambda n: [refs.pop(0) for _ in range(n)]
    longs = take(ring - 1)
    shorts = take(ring - 1) if 1 in which else []
    others = dict(zip(which, take(len(which))))
    early, late = take(len(which)), take(len(which))
    new_ref = take(1)[0]
    sums_ref, left_here, right_here, sems, *staged = refs
    if staged:
        *held, more_sems = staged
        sources = longs + shorts + list(others.values())
        arrivals = [pltpu.make_async_copy(a, b, more_sems.at[i]) for i, (a, b) in enumerate(zip(sources, held))]
        for copy in arrivals:
            copy.start()
        longs, shorts = held[: len(longs)], held[len(longs) : len(longs) + len(shorts)]
        others = dict(zip(which, held[len(longs) + len(shorts) :]))
    copies = fetch(ring, own, left, right, left_here, right_here, sems)
    rows, part = late[0].shape[0], late[0].shape[1] // 2
    new = {}
    for w, block, term in zip(which, early, late):
        facts = block.at[rows : rows + EXTRA]
        updated = block[0:rows, :] - 0.7 * term[...] / denominators(facts, rows)
        value = jnp.where(inside(facts, rows, part, w), updated, 0.0)
        mine, yours = columns(part, w)
        new_ref[:, mine] = value[:, 0:part]
        new_ref[:, yours] = value[:, part:]
        new[w] = halves(value)

    if staged:
        for copy in arrivals:
            copy.wait()

    def add_up(spot, lefts, rights):
        product = None
        for w, value in new.items():
            term = dot3(value, halves(rights(w)), NN)
            product = term if product is None else product + term
        sums_ref[spot : spot + 1, :] = jnp.sum(lefts * product, axis=0, keepdims=True)

    for i, long in enumerate(longs):
        add_up(
            i + 1,
            long[0:rows, :],
            lambda w: jnp.concatenate([long[rows:, :] if w == 0 else shorts[i][...], others[w][i]], axis=0),
        )
    for copy in copies:
        copy.wait()
    add_up(0, left_here[...], lambda w: jnp.concatenate([right_here[spot, :] for spot in columns(part, w)], axis=0))


def density_first_kernel(ring, own, left, right, *refs):
    *packs, block, term, later_term, sums_ref, top_ref, low_ref, own_left, base_ref, keep_ref, right_here, sems = refs
    longs, shorts, (others, later_others) = packs[: ring - 1], packs[ring - 1 : 2 * ring - 2], packs[2 * ring - 2 :]
    copies = fetch(ring, own, left, right, own_left, right_here, sems)
    rows, part = term.shape[0], term.shape[1] // 2
    facts = block.at[rows : rows + EXTRA]
    updated = block[0:rows, :] - 0.7 * term[...] / denominators(facts, rows)
    value = halves(jnp.where(inside(facts, rows, part, 0), updated, 0.0))
    base_ref[...] = 0.7 * later_term[...] / denominators(facts, rows, 4)
    keep_ref[...] = jnp.where(inside(facts, rows, part, 1), 1.0, 0.0)

    def prepare(spot, mine, yours):
        for i, source in enumerate((mine, yours)):
            top_ref[spot, i * part : (i + 1) * part, :], low_ref[spot, i * part : (i + 1) * part, :] = halves(source)

    def add_up(spot, lefts, mine, yours):
        product = dot3(value, halves(jnp.concatenate([mine, yours], axis=0)), NN)
        sums_ref[spot : spot + 1, :] = jnp.sum(lefts * product, axis=0, keepdims=True)

    for i, (long, short) in enumerate(zip(longs, shorts)):
        add_up(i + 1, long[0:rows, :], long[rows:, :], others[i])
        prepare(i + 1, short[...], later_others[i])
    for copy in copies:
        copy.wait()
    add_up(0, own_left[...], *[right_here[spot, :] for spot in columns(part, 0)])
    prepare(0, *[right_here[spot, :] for spot in columns(part, 1)])


def density_last_kernel(block, base, keep, top, low, own_left, *refs):
    *longs, before, sums_ref = refs
    rows = base.shape[0]
    value = halves(jnp.where(keep[...] > 0.0, block[0:rows, :] - base[...], 0.0))
    for spot, long in enumerate((own_left, *longs)):
        product = dot3(value, (top[spot], low[spot]), NN)
        sums_ref[spot : spot + 1, :] = before[spot : spot + 1, :] + jnp.sum(long[0:rows, :] * product, axis=0, keepdims=True)


def correction_kernel(pairs_per_shard, shards, neighbours, coupling, mixed, up, down, wrap, far, d_ref, out_ref):
    shard = lax.axis_index("pair")

    def weight(by):
        total = jnp.float32(0)
        for k in range(neighbours.shape[0]):
            apart = (neighbours[k] // pairs_per_shard - shard + shards) % shards
            total += jnp.where(apart == by, coupling[k], 0.0)
        return total

    above, below = weight(1), weight(shards - 1)
    spot = shard % SEGMENT
    ends = jnp.where(spot == SEGMENT - 1, above, jnp.where(spot == 0, below, 0.0))
    total = weight(0) * mixed[...] + above * up[...] + below * down[...]
    total += ends * wrap[...] + weight(shards // 2) * far[...]
    out_ref[...] = dot3(halves(total), halves(d_ref[...]), NN)


def vmem(*arrays):
    return [pltpu.with_memory_space_constraint(a, pltpu.VMEM) for a in arrays]


def hbm(*arrays):
    return [pltpu.with_memory_space_constraint(a, pltpu.HBM) for a in arrays]


def cost(flops, moved):
    return pl.CostEstimate(flops=flops, bytes_accessed=moved, transcendentals=0)


def body(left, right, amplitudes, domain_trans, vir_energy, occ_energy, coupling, neighbours, dom_blocks):
    fit_count, pair_count = lax.axis_size("fit"), lax.axis_size("pair")
    ring = fit_count // 2
    rows, width, depth = left.shape[1], right.shape[1], left.shape[2]
    fit = lax.axis_index("fit")
    side, place = fit // ring, fit % ring
    amp, trans = amplitudes[0], domain_trans[0]
    swap = [(0, 1), (1, 0)]
    across = [(f, (f + ring) % fit_count) for f in range(fit_count)]
    block = jax.ShapeDtypeStruct((rows, width), F32)
    sums = jax.ShapeDtypeStruct((ring, depth), F32)

    def shifted(by):
        return [(s * ring + i, s * ring + (i + by) % ring) for s in range(2) for i in range(ring)]

    def send(value, axis, pairs):
        return lax.ppermute(value, axis, pairs)

    def from_shards(value, sources):
        return send(value, "pair", [(source % pair_count, to) for to, source in sources])

    part = width // 4
    packs = [jax.ShapeDtypeStruct((rows + part, depth), F32)] * (ring - 1) + [jax.ShapeDtypeStruct((part, depth), F32)] * (ring - 1)
    pack_sems = pltpu.SemaphoreType.DMA((ring - 1, 3))
    some = jax.ShapeDtypeStruct((rows, 2 * part), F32)
    some_long = jax.ShapeDtypeStruct((rows + EXTRA, 2 * part), F32)
    edge = jax.ShapeDtypeStruct((ring - 1, part, depth), F32)

    def spread(values):
        return [send(value, "fit", shifted(by)) for by, value in enumerate(values, 1)]

    def swapped(values):
        gathered = pl.pallas_call(
            gather_kernel,
            in_specs=[WHOLE] * len(values),
            out_specs=WHOLE,
            out_shape=edge,
            compiler_params=LIMIT,
            cost_estimate=cost(0, 8 * edge.size),
        )(*vmem(*values))
        return gathered, send(gathered, "blk", swap)

    def work(kernel, own, which, factors, extras, outs, resident=True):
        held = [pltpu.VMEM(a.shape, F32) for a in factors] + [pltpu.SemaphoreType.DMA((len(factors),))]
        return pl.pallas_call(
            functools.partial(kernel, ring, own, which),
            in_specs=[ANY] * 2 + [WHOLE if resident else ANY] * len(factors) + [WHOLE] * len(extras),
            out_specs=[WHOLE] * len(outs),
            out_shape=outs,
            scratch_shapes=[
                pltpu.VMEM((rows, depth), F32),
                pltpu.VMEM((width, depth), F32),
                pltpu.SemaphoreType.DMA((2,)),
                *([] if resident else held),
            ],
            compiler_params=LIMIT,
            cost_estimate=cost(3 * rows * width * depth * ring, 2 * ring * depth * (rows + width)),
        )(*hbm(left, right), *(vmem if resident else hbm)(*factors), *vmem(*extras))

    *sent, mixed = pl.pallas_call(
        functools.partial(head_kernel, ring),
        in_specs=[ANY] * 4,
        out_specs=[WHOLE] * (2 * ring - 1),
        out_shape=packs + [block],
        scratch_shapes=[pltpu.VMEM(amp.shape, F32), pltpu.VMEM(trans.shape, F32), pack_sems, pltpu.SemaphoreType.DMA((2,))],
        compiler_params=LIMIT,
        cost_estimate=cost(6 * rows * width * width, 32 * rows * width),
    )(*hbm(left, right, amp, trans))
    their_longs, their_shorts = spread(sent[: ring - 1]), spread(sent[ring - 1 :])
    shards = range(pair_count)
    near = [
        from_shards(mixed, [(s, s + 1) for s in shards if s % SEGMENT < SEGMENT - 1]),
        from_shards(mixed, [(s, s - 1) for s in shards if s % SEGMENT > 0]),
        from_shards(mixed, [(s, s + 1) for s in shards if s % SEGMENT == SEGMENT - 1] + [(s, s - 1) for s in shards if s % SEGMENT == 0]),
        from_shards(mixed, [(s, s + pair_count // 2) for s in shards]),
    ]
    *sent, facts = pl.pallas_call(
        functools.partial(pack_kernel, ring, True),
        in_specs=[SCALARS] * 2 + [ANY] * 2 + [WHOLE, ANY],
        out_specs=[WHOLE] * (1 + len(packs)),
        out_shape=packs + [jax.ShapeDtypeStruct((2, EXTRA, 2 * part), F32)],
        scratch_shapes=[pack_sems],
        compiler_params=LIMIT,
        cost_estimate=cost(0, 24 * rows * width),
    )(occ_energy, dom_blocks, *hbm(left, right), vir_energy, mixed)
    my_longs, my_shorts = spread(sent[: ring - 1]), spread(sent[ring - 1 :])
    (corr,) = pl.pallas_call(
        functools.partial(correction_kernel, fit_count, pair_count),
        in_specs=[SCALARS] * 2 + [WHOLE] * 6,
        out_specs=[WHOLE],
        out_shape=[block],
        compiler_params=LIMIT,
        cost_estimate=cost(6 * rows * width * width, 28 * rows * width),
    )(neighbours[0], coupling[0], mixed, *near, trans)

    their_others, their_parts, my_late = [], [], []
    for which, source in enumerate((their_longs, their_shorts)):
        gathered, other = swapped(source)
        (started,) = work(integral_kernel, False, which, (*their_longs, gathered), (), [some])
        done = pl.pallas_call(
            finish_kernel,
            in_specs=[WHOLE] * (2 + len(their_longs)),
            out_specs=WHOLE,
            out_shape=some,
            compiler_params=LIMIT,
            cost_estimate=cost(2 * rows * width * depth, 16 * rows * width),
        )(started, *vmem(*their_longs, other))
        their_others.append(other)
        their_parts.append(done)
        my_late.append(send(done, "fit", across))
    my_others, my_early, their_early = [], [], []
    for which, source in enumerate((my_longs, my_shorts)):
        gathered, other = swapped(source)
        (started,) = work(integral_kernel, True, which, (*my_longs, gathered), (), [some])
        done = pl.pallas_call(
            functools.partial(residual_kernel, which),
            in_specs=[WHOLE] * (5 + len(my_longs)),
            out_specs=WHOLE,
            out_shape=some_long,
            compiler_params=LIMIT,
            cost_estimate=cost(2 * rows * width * depth, 24 * rows * width),
        )(started, *vmem(*my_longs, other), amp, corr, facts)
        my_others.append(other)
        my_early.append(done)
        their_early.append(send(done, "fit", across))
    new, my_sums = work(
        density_kernel, True, (0, 1), (*my_longs, *my_shorts, *my_others), (*my_early, *my_late), [block, sums], resident=False
    )
    square = jax.ShapeDtypeStruct((rows, depth), F32)
    ready = jax.ShapeDtypeStruct((ring, 2 * part, depth), jnp.bfloat16)
    their_sums, top, low, own_left, base, keep = pl.pallas_call(
        functools.partial(density_first_kernel, ring, False),
        in_specs=[ANY] * 2 + [WHOLE] * (2 * ring + 3),
        out_specs=[WHOLE] * 6,
        out_shape=[sums, ready, ready, square, some, some],
        scratch_shapes=[pltpu.VMEM((width, depth), F32), pltpu.SemaphoreType.DMA((2,))],
        compiler_params=LIMIT,
        cost_estimate=cost(3 * rows * width * depth * ring, 2 * ring * depth * (rows + width)),
    )(*hbm(left, right), *vmem(*their_longs, *their_shorts, *their_others, their_early[0], *their_parts))
    their_sums = pl.pallas_call(
        density_last_kernel,
        in_specs=[WHOLE] * (ring + 6),
        out_specs=WHOLE,
        out_shape=sums,
        compiler_params=LIMIT,
        cost_estimate=cost(3 * rows * width * depth * ring, ring * depth * (rows + width)),
    )(*vmem(their_early[1], base, keep, top, low, own_left, *their_longs, their_sums))
    both = jnp.stack([my_sums, their_sums], axis=1)
    both = both + lax.ppermute(both, "blk", swap)
    parts = [both[0]] + [lax.ppermute(both[by], "fit", shifted(-by)) for by in range(1, ring)]
    density = jnp.zeros((2, ring, depth), F32)
    for by, part in enumerate(parts):
        at = (place + by) % ring
        density = jnp.where((jnp.arange(ring) == at)[None, :, None], part[:, None, :], density)
    density = jnp.where(side == 0, density, density[::-1])
    return new[None], density.reshape(fit_count, depth)


def solution(mesh):
    placed = (
        P("pair", "blk", "fit"),
        P("pair", None, "fit"),
        P(("pair", "fit"), "blk", None),
        P(("pair", "fit"), None, None),
        P(("pair", "fit"), None),
        P(("pair", "fit")),
        P(("pair", "fit"), None),
        P(("pair", "fit"), None),
        P(("pair", "fit")),
    )
    return jax.shard_map(
        lambda *args: body(*args),
        mesh=mesh,
        in_specs=placed,
        out_specs=(P(("pair", "fit"), "blk", None), P("pair", "fit")),
        check_vma=False,
    )
```

```python
import functools

import jax
import jax.numpy as jnp
from jax import lax
from jax.experimental import pallas as pl
from jax.experimental.pallas import tpu as pltpu
from jax.sharding import PartitionSpec as P


F32 = jnp.float32
NT = (((1,), (1,)), ((), ()))
NN = (((1,), (0,)), ((), ()))
ANY = pl.BlockSpec(memory_space=pltpu.HBM)
SCALARS = pl.BlockSpec(memory_space=pltpu.SMEM)
WHOLE = pl.BlockSpec(memory_space=pltpu.VMEM)
LIMIT = pltpu.CompilerParams(vmem_limit_bytes=16 << 20)
EXTRA = 8


def halves(v):
    top = v.astype(jnp.bfloat16)
    return top, (v - top.astype(F32)).astype(jnp.bfloat16)


def dot3(a, b, dims):
    a_top, a_low = a
    b_top, b_low = b
    dot = functools.partial(lax.dot_general, dimension_numbers=dims, preferred_element_type=F32)
    return (dot(a_low, b_top) + dot(a_top, b_low)) + dot(a_top, b_top)


def seat(ring, own):
    fit = lax.axis_index("fit")
    side = fit // ring
    return fit % ring, (side if own else 1 - side) * ring


def fill_packs(ring, own, left, right, outs, sems):
    place, first = seat(ring, own)
    rows = left.shape[1]
    half = right.shape[1] // 2
    part = half // 2
    start = lax.axis_index("blk") * half
    copies = []
    for by in range(1, ring):
        slot = first + (place + by) % ring
        long, short = outs[by - 1], outs[ring - 2 + by]
        for i, (source, to) in enumerate((
            (left.at[slot], long.at[0:rows]),
            (right.at[slot, pl.ds(pl.multiple_of(start, part), part)], long.at[rows : rows + part]),
            (right.at[slot, pl.ds(pl.multiple_of(start + part, part), part)], short),
        )):
            copies.append(pltpu.make_async_copy(source, to, sems.at[by - 1, i]))
    for copy in copies:
        copy.start()
    return copies


def pack_kernel(ring, own, occ, dom, left, right, vir, _, *refs):
    *packs, facts, sems = refs
    copies = fill_packs(ring, own, left, right, packs, sems)
    rows, width = left.shape[1], vir.shape[1]
    part = width // 4
    core = lax.axis_index("blk")
    for which in range(facts.shape[0]):
        facts[which] = jnp.concatenate([
            jnp.concatenate([vir[:, spot] for spot in columns(part, which)], axis=1),
            vir[:, pl.ds(pl.multiple_of(core * rows, rows), rows)],
            jnp.full((1, 2 * part), occ[0], F32),
            jnp.full((1, 2 * part), (dom[0] * part).astype(F32), F32),
            jnp.concatenate([vir[:, spot] for spot in columns(part, 1)], axis=1),
            jnp.zeros((EXTRA - 5, 2 * part), F32),
        ])
    for copy in copies:
        copy.wait()


def head_kernel(ring, left, right, amp, trans, *refs):
    *packs, mixed, amp_here, trans_here, sems, own_sems = refs
    reads = [
        pltpu.make_async_copy(amp, amp_here, own_sems.at[0]),
        pltpu.make_async_copy(trans, trans_here, own_sems.at[1]),
    ]
    for read in reads:
        read.start()
    copies = fill_packs(ring, False, left, right, packs, sems)
    for read in reads:
        read.wait()
    mixed[...] = dot3(halves(amp_here[...]), halves(trans_here[...]), NT)
    for copy in copies:
        copy.wait()


def gather_kernel(*refs):
    *sources, out_ref = refs
    part = out_ref.shape[1]
    for i, source in enumerate(sources):
        out_ref[i] = source[source.shape[0] - part :, :]


def fetch(ring, own, left, right, left_here, right_here, sems):
    place, first = seat(ring, own)
    copies = [
        pltpu.make_async_copy(left.at[first + place], left_here, sems.at[0]),
        pltpu.make_async_copy(right.at[first + place], right_here, sems.at[1]),
    ]
    for copy in copies:
        copy.start()
    return copies


def columns(part, which):
    core = lax.axis_index("blk")
    return [pl.ds(pl.multiple_of((2 * c + which) * part, part), part) for c in (core, 1 - core)]


def integral_kernel(ring, own, which, left, right, *refs):
    (*packs, rights, out_ref, left_here, right_here, sems) = refs
    copies = fetch(ring, own, left, right, left_here, right_here, sems)
    rows = left_here.shape[0]
    part = rights.shape[1]
    total = None
    for i, pack in enumerate(packs):
        term = dot3(halves(pack[0:rows, :]), halves(rights[i]), NT)
        total = term if total is None else total + term
    for copy in copies:
        copy.wait()
    own_left = halves(left_here[...])
    mine, yours = columns(part, which)
    out_ref[:, 0:part] = total + dot3(own_left, halves(right_here[mine, :]), NT)
    out_ref[:, part:] = dot3(own_left, halves(right_here[yours, :]), NT)


def finished(part_ref, packs, others):
    rows, part = part_ref.shape[0], others.shape[1]
    total = part_ref[:, part:]
    for i, pack in enumerate(packs):
        total += dot3(halves(pack[0:rows, :]), halves(others[i]), NT)
    return jnp.concatenate([part_ref[:, 0:part], total], axis=1)


def finish_kernel(part_ref, *refs):
    *packs, others, out_ref = refs
    out_ref[...] = finished(part_ref, packs, others)


def denominators(facts, rows, at=0):
    width = facts.shape[1]
    column = jnp.broadcast_to(facts[1:2, 0:rows], (128, rows)).T
    return jnp.concatenate([column] * (width // 128), axis=1) + facts[at : at + 1, :] + facts[2:3, 0:1]


def inside(facts, rows, part, which):
    core = lax.axis_index("blk")
    row = (core * rows + lax.broadcasted_iota(jnp.int32, (rows, 2 * part), 0)).astype(F32)
    lane = lax.broadcasted_iota(jnp.int32, (rows, 2 * part), 1)
    offset = jnp.where(lane < part, 2 * core * part, (1 - 2 * core) * part) + which * part
    limit = facts[3:4, 0:1]
    return (row < limit) & ((lane + offset).astype(F32) < limit)


def residual_kernel(which, part_ref, *refs):
    *packs, others, amp, corr, facts, out_ref = refs
    rows = amp.shape[0]
    spots = columns(others.shape[1], which)
    out_ref[rows:, :] = facts[which]
    below = denominators(facts.at[which], rows)
    old = jnp.concatenate([amp[:, spot] for spot in spots], axis=1)
    fixed = below * old - jnp.concatenate([corr[:, spot] for spot in spots], axis=1)
    residual = finished(part_ref, packs, others) + fixed
    out_ref[0:rows, :] = old - 0.7 * residual / below


def density_kernel(ring, own, which, left, right, *refs):
    refs = list(refs)
    take = lambda n: [refs.pop(0) for _ in range(n)]
    longs = take(ring - 1)
    shorts = take(ring - 1) if 1 in which else []
    others = dict(zip(which, take(len(which))))
    early, late = take(len(which)), take(len(which))
    new_ref = take(1)[0]
    sums_ref, left_here, right_here, sems, *staged = refs
    if staged:
        *held, more_sems = staged
        sources = longs + shorts + list(others.values())
        arrivals = [pltpu.make_async_copy(a, b, more_sems.at[i]) for i, (a, b) in enumerate(zip(sources, held))]
        for copy in arrivals:
            copy.start()
        longs, shorts = held[: len(longs)], held[len(longs) : len(longs) + len(shorts)]
        others = dict(zip(which, held[len(longs) + len(shorts) :]))
    copies = fetch(ring, own, left, right, left_here, right_here, sems)
    rows, part = late[0].shape[0], late[0].shape[1] // 2
    new = {}
    for w, block, term in zip(which, early, late):
        facts = block.at[rows : rows + EXTRA]
        updated = block[0:rows, :] - 0.7 * term[...] / denominators(facts, rows)
        value = jnp.where(inside(facts, rows, part, w), updated, 0.0)
        mine, yours = columns(part, w)
        new_ref[:, mine] = value[:, 0:part]
        new_ref[:, yours] = value[:, part:]
        new[w] = halves(value)

    if staged:
        for copy in arrivals:
            copy.wait()

    def add_up(spot, lefts, rights):
        product = None
        for w, value in new.items():
            term = dot3(value, halves(rights(w)), NN)
            product = term if product is None else product + term
        sums_ref[spot : spot + 1, :] = jnp.sum(lefts * product, axis=0, keepdims=True)

    for i, long in enumerate(longs):
        add_up(
            i + 1,
            long[0:rows, :],
            lambda w: jnp.concatenate([long[rows:, :] if w == 0 else shorts[i][...], others[w][i]], axis=0),
        )
    for copy in copies:
        copy.wait()
    add_up(0, left_here[...], lambda w: jnp.concatenate([right_here[spot, :] for spot in columns(part, w)], axis=0))


def density_first_kernel(ring, own, left, right, *refs):
    *packs, block, term, later_term, sums_ref, top_ref, low_ref, own_left, base_ref, keep_ref, right_here, sems = refs
    longs, shorts, (others, later_others) = packs[: ring - 1], packs[ring - 1 : 2 * ring - 2], packs[2 * ring - 2 :]
    copies = fetch(ring, own, left, right, own_left, right_here, sems)
    rows, part = term.shape[0], term.shape[1] // 2
    facts = block.at[rows : rows + EXTRA]
    updated = block[0:rows, :] - 0.7 * term[...] / denominators(facts, rows)
    value = halves(jnp.where(inside(facts, rows, part, 0), updated, 0.0))
    base_ref[...] = 0.7 * later_term[...] / denominators(facts, rows, 4)
    keep_ref[...] = jnp.where(inside(facts, rows, part, 1), 1.0, 0.0)

    def prepare(spot, mine, yours):
        for i, source in enumerate((mine, yours)):
            top_ref[spot, i * part : (i + 1) * part, :], low_ref[spot, i * part : (i + 1) * part, :] = halves(source)

    def add_up(spot, lefts, mine, yours):
        product = dot3(value, halves(jnp.concatenate([mine, yours], axis=0)), NN)
        sums_ref[spot : spot + 1, :] = jnp.sum(lefts * product, axis=0, keepdims=True)

    for i, (long, short) in enumerate(zip(longs, shorts)):
        add_up(i + 1, long[0:rows, :], long[rows:, :], others[i])
        prepare(i + 1, short[...], later_others[i])
    for copy in copies:
        copy.wait()
    add_up(0, own_left[...], *[right_here[spot, :] for spot in columns(part, 0)])
    prepare(0, *[right_here[spot, :] for spot in columns(part, 1)])


def density_last_kernel(block, base, keep, top, low, own_left, *refs):
    *longs, before, sums_ref = refs
    rows = base.shape[0]
    value = halves(jnp.where(keep[...] > 0.0, block[0:rows, :] - base[...], 0.0))
    for spot, long in enumerate((own_left, *longs)):
        product = dot3(value, (top[spot], low[spot]), NN)
        sums_ref[spot : spot + 1, :] = before[spot : spot + 1, :] + jnp.sum(long[0:rows, :] * product, axis=0, keepdims=True)


def correction_kernel(pairs_per_shard, shards, neighbours, coupling, mixed, first, second, far, d_ref, out_ref):
    shard = lax.axis_index("pair")

    def weight(by):
        total = jnp.float32(0)
        for k in range(neighbours.shape[0]):
            apart = (neighbours[k] // pairs_per_shard - shard + shards) % shards
            total += jnp.where(apart == by, coupling[k], 0.0)
        return total

    above, below = weight(1), weight(shards - 1)
    even = shard % 2 == 0
    total = weight(0) * mixed[...] + jnp.where(even, above, below) * first[...]
    total += jnp.where(even, below, above) * second[...] + weight(shards // 2) * far[...]
    out_ref[...] = dot3(halves(total), halves(d_ref[...]), NN)


def seat_kernel(ring, *refs):
    *parts, out_ref = refs
    place, first = seat(ring, True)
    for by, part in enumerate(parts):
        at = (place + by) % ring
        out_ref[pl.ds(first + at, 1), :] = part[0:1, :]
        out_ref[pl.ds(ring - first + at, 1), :] = part[1:2, :]


def vmem(*arrays):
    return [pltpu.with_memory_space_constraint(a, pltpu.VMEM) for a in arrays]


def hbm(*arrays):
    return [pltpu.with_memory_space_constraint(a, pltpu.HBM) for a in arrays]


def cost(flops, moved):
    return pl.CostEstimate(flops=flops, bytes_accessed=moved, transcendentals=0)


def body(left, right, amplitudes, domain_trans, vir_energy, occ_energy, coupling, neighbours, dom_blocks):
    fit_count, pair_count = lax.axis_size("fit"), lax.axis_size("pair")
    ring = fit_count // 2
    rows, width, depth = left.shape[1], right.shape[1], left.shape[2]
    amp, trans = amplitudes[0], domain_trans[0]
    swap = [(0, 1), (1, 0)]
    across = [(f, (f + ring) % fit_count) for f in range(fit_count)]
    block = jax.ShapeDtypeStruct((rows, width), F32)
    sums = jax.ShapeDtypeStruct((ring, depth), F32)

    def shifted(by):
        return [(s * ring + i, s * ring + (i + by) % ring) for s in range(2) for i in range(ring)]

    def send(value, axis, pairs):
        return lax.ppermute(value, axis, pairs)

    def from_shards(value, sources):
        return send(value, "pair", [(source % pair_count, to) for to, source in sources])

    part = width // 4
    packs = [jax.ShapeDtypeStruct((rows + part, depth), F32)] * (ring - 1) + [jax.ShapeDtypeStruct((part, depth), F32)] * (ring - 1)
    pack_sems = pltpu.SemaphoreType.DMA((ring - 1, 3))
    some = jax.ShapeDtypeStruct((rows, 2 * part), F32)
    some_long = jax.ShapeDtypeStruct((rows + EXTRA, 2 * part), F32)
    edge = jax.ShapeDtypeStruct((ring - 1, part, depth), F32)

    def spread(values):
        return [send(value, "fit", shifted(by)) for by, value in enumerate(values, 1)]

    def swapped(values):
        gathered = pl.pallas_call(
            gather_kernel,
            in_specs=[WHOLE] * len(values),
            out_specs=WHOLE,
            out_shape=edge,
            compiler_params=LIMIT,
            cost_estimate=cost(0, 8 * edge.size),
        )(*vmem(*values))
        return gathered, send(gathered, "blk", swap)

    def work(kernel, own, which, factors, extras, outs, resident=True):
        held = [pltpu.VMEM(a.shape, F32) for a in factors] + [pltpu.SemaphoreType.DMA((len(factors),))]
        return pl.pallas_call(
            functools.partial(kernel, ring, own, which),
            in_specs=[ANY] * 2 + [WHOLE if resident else ANY] * len(factors) + [WHOLE] * len(extras),
            out_specs=[WHOLE] * len(outs),
            out_shape=outs,
            scratch_shapes=[
                pltpu.VMEM((rows, depth), F32),
                pltpu.VMEM((width, depth), F32),
                pltpu.SemaphoreType.DMA((2,)),
                *([] if resident else held),
            ],
            compiler_params=LIMIT,
            cost_estimate=cost(3 * rows * width * depth * ring, 2 * ring * depth * (rows + width)),
        )(*hbm(left, right), *(vmem if resident else hbm)(*factors), *vmem(*extras))

    *sent, mixed = pl.pallas_call(
        functools.partial(head_kernel, ring),
        in_specs=[ANY] * 4,
        out_specs=[WHOLE] * (2 * ring - 1),
        out_shape=packs + [block],
        scratch_shapes=[pltpu.VMEM(amp.shape, F32), pltpu.VMEM(trans.shape, F32), pack_sems, pltpu.SemaphoreType.DMA((2,))],
        compiler_params=LIMIT,
        cost_estimate=cost(6 * rows * width * width, 32 * rows * width),
    )(*hbm(left, right, amp, trans))
    their_longs, their_shorts = spread(sent[: ring - 1]), spread(sent[ring - 1 :])
    shards = range(pair_count)
    near = [
        from_shards(mixed, [(s, s + 1 - 2 * (s % 2)) for s in shards]),
        from_shards(mixed, [(s, s - 1 + 2 * (s % 2)) for s in shards]),
        from_shards(mixed, [(s, s + pair_count // 2) for s in shards]),
    ]
    *sent, facts = pl.pallas_call(
        functools.partial(pack_kernel, ring, True),
        in_specs=[SCALARS] * 2 + [ANY] * 2 + [WHOLE, ANY],
        out_specs=[WHOLE] * (1 + len(packs)),
        out_shape=packs + [jax.ShapeDtypeStruct((2, EXTRA, 2 * part), F32)],
        scratch_shapes=[pack_sems],
        compiler_params=LIMIT,
        cost_estimate=cost(0, 24 * rows * width),
    )(occ_energy, dom_blocks, *hbm(left, right), vir_energy, mixed)
    my_longs, my_shorts = spread(sent[: ring - 1]), spread(sent[ring - 1 :])
    (corr,) = pl.pallas_call(
        functools.partial(correction_kernel, fit_count, pair_count),
        in_specs=[SCALARS] * 2 + [WHOLE] * 5,
        out_specs=[WHOLE],
        out_shape=[block],
        compiler_params=LIMIT,
        cost_estimate=cost(6 * rows * width * width, 28 * rows * width),
    )(neighbours[0], coupling[0], mixed, *near, trans)

    their_others, their_parts, my_late = [], [], []
    for which, source in enumerate((their_longs, their_shorts)):
        gathered, other = swapped(source)
        (started,) = work(integral_kernel, False, which, (*their_longs, gathered), (), [some])
        done = pl.pallas_call(
            finish_kernel,
            in_specs=[WHOLE] * (2 + len(their_longs)),
            out_specs=WHOLE,
            out_shape=some,
            compiler_params=LIMIT,
            cost_estimate=cost(2 * rows * width * depth, 16 * rows * width),
        )(started, *vmem(*their_longs, other))
        their_others.append(other)
        their_parts.append(done)
        my_late.append(send(done, "fit", across))
    my_others, my_early, their_early = [], [], []
    for which, source in enumerate((my_longs, my_shorts)):
        gathered, other = swapped(source)
        (started,) = work(integral_kernel, True, which, (*my_longs, gathered), (), [some])
        done = pl.pallas_call(
            functools.partial(residual_kernel, which),
            in_specs=[WHOLE] * (5 + len(my_longs)),
            out_specs=WHOLE,
            out_shape=some_long,
            compiler_params=LIMIT,
            cost_estimate=cost(2 * rows * width * depth, 24 * rows * width),
        )(started, *vmem(*my_longs, other), amp, corr, facts)
        my_others.append(other)
        my_early.append(done)
        their_early.append(send(done, "fit", across))
    new, my_sums = work(
        density_kernel, True, (0, 1), (*my_longs, *my_shorts, *my_others), (*my_early, *my_late), [block, sums], resident=False
    )
    square = jax.ShapeDtypeStruct((rows, depth), F32)
    ready = jax.ShapeDtypeStruct((ring, 2 * part, depth), jnp.bfloat16)
    their_sums, top, low, own_left, base, keep = pl.pallas_call(
        functools.partial(density_first_kernel, ring, False),
        in_specs=[ANY] * 2 + [WHOLE] * (2 * ring + 3),
        out_specs=[WHOLE] * 6,
        out_shape=[sums, ready, ready, square, some, some],
        scratch_shapes=[pltpu.VMEM((width, depth), F32), pltpu.SemaphoreType.DMA((2,))],
        compiler_params=LIMIT,
        cost_estimate=cost(3 * rows * width * depth * ring, 2 * ring * depth * (rows + width)),
    )(*hbm(left, right), *vmem(*their_longs, *their_shorts, *their_others, their_early[0], *their_parts))
    their_sums = pl.pallas_call(
        density_last_kernel,
        in_specs=[WHOLE] * (ring + 6),
        out_specs=WHOLE,
        out_shape=sums,
        compiler_params=LIMIT,
        cost_estimate=cost(3 * rows * width * depth * ring, ring * depth * (rows + width)),
    )(*vmem(their_early[1], base, keep, top, low, own_left, *their_longs, their_sums))
    both = jnp.stack([my_sums, their_sums], axis=1)
    both = both + lax.ppermute(both, "blk", swap)
    parts = [both[0]] + [lax.ppermute(both[by], "fit", shifted(-by)) for by in range(1, ring)]
    density = pl.pallas_call(
        functools.partial(seat_kernel, ring),
        in_specs=[WHOLE] * ring,
        out_specs=WHOLE,
        out_shape=jax.ShapeDtypeStruct((fit_count, depth), F32),
        compiler_params=LIMIT,
        cost_estimate=cost(0, 8 * fit_count * depth),
    )(*parts)
    return new[None], density


def solution(mesh):
    placed = (
        P("pair", "blk", "fit"),
        P("pair", None, "fit"),
        P(("pair", "fit"), "blk", None),
        P(("pair", "fit"), None, None),
        P(("pair", "fit"), None),
        P(("pair", "fit")),
        P(("pair", "fit"), None),
        P(("pair", "fit"), None),
        P(("pair", "fit")),
    )
    return jax.shard_map(
        lambda *args: body(*args),
        mesh=mesh,
        in_specs=placed,
        out_specs=(P(("pair", "fit"), "blk", None), P("pair", "fit")),
        check_vma=False,
    )
```
